256 devices in a mesh: section: 8 (over z_lo, core), band: 32 (over x, z_hi, y).
Axes of the slice: x: 4, y: 4, z: 8 (z_hi: 2, z_lo: 4; z = z_hi * 4 + z_lo), core: 2. Of those that a mesh axis runs over, the one named last changes fastest.
Arguments:
- image: bfloat16 [64, 160, 320], P('band'), may hold values from -6 to 6
- carried: bfloat16 [8, 64, 160, 320], P('section', 'band'), may hold values from -6 to 6
- saved: bfloat16 [8, 64, 160, 320], P('section', 'band'), may hold values from -6 to 6
- sent_grad: bfloat16 [8, 64, 160, 320], P('section', 'band'), may hold values from -6 to 6
- loss_grad: bfloat16 [64, 160, 320], P('band'), may hold values from -6 to 6
- first_kernel: bfloat16 [8, 2880, 320], P('section'), may hold values from -0.109375 to 0.109375
- second_kernel: bfloat16 [8, 2880, 320], P('section'), may hold values from -0.109375 to 0.109375
Outputs:
- forward_out: bfloat16 [8, 64, 160, 320], P('section', 'band')
- input_grad: bfloat16 [8, 64, 160, 320], P('section', 'band')
- first_kernel_grad: float32 [8, 2880, 320], P('section', 'band')
- second_kernel_grad: float32 [8, 2880, 320], P('section', 'band')
The draws below stay inside these ranges and needn't reach their ends.
All inputs are finite; a program needn't handle non-finite values.
Results may differ from the reference program's by a relative error of at most 0.0033.
Values may be sent and summed in bfloat16 or wider, within the bound.
A program may use at most 128 MiB of HBM per device.

```python
import jax
import jax.numpy as jnp
from jax import lax

C = 320
COLS = 160
SECTIONS = 8
NROWS = 64


def shard_levels(own_key, dims, shards, least, high):
    level = 1.0
    for position, blocks in shards:
        draws = jax.random.uniform(jax.random.fold_in(jax.random.fold_in(own_key, 6), position), (blocks,), jnp.float32, least / len(shards), high / len(shards))
        level = level * jnp.repeat(jnp.exp(draws), dims[position] // blocks).reshape((-1,) + (1,) * (len(dims) - 1 - position))
    return level


def bell_draw(stream_key, extent, deviation, limit, cuts=(), held_as=jnp.bfloat16):
    factor_of = shard_levels(stream_key, extent, cuts, -0.22, 0.18) if cuts else 1.0
    drawn = jax.random.normal(stream_key, extent, jnp.float32) * deviation * factor_of
    return jnp.minimum(jnp.maximum(drawn, -limit), limit).astype(held_as)


def setup_inputs(seed: int = 0) -> dict:
    keys = jax.random.split(jax.random.key(seed), 8)
    return {
        "image": bell_draw(keys[0], (NROWS, COLS, C), 1.0, 6.0, ((0, 32),)),
        "carried": bell_draw(keys[1], (SECTIONS, NROWS, COLS, C), 1.0, 6.0, ((0, 8), (1, 32))),
        "saved": bell_draw(keys[2], (SECTIONS, NROWS, COLS, C), 1.0, 6.0, ((0, 8), (1, 32))),
        "sent_grad": bell_draw(keys[3], (SECTIONS, NROWS, COLS, C), 1.0, 6.0, ((0, 8), (1, 32))),
        "loss_grad": bell_draw(keys[4], (NROWS, COLS, C), 1.0, 6.0, ((0, 32),)),
        "first_kernel": bell_draw(keys[5], (SECTIONS, 9 * C, C), (9 * C) ** -0.5, 0.109375, ((0, 8),)),
        "second_kernel": bell_draw(keys[6], (SECTIONS, 9 * C, C), (9 * C) ** -0.5, 0.109375, ((0, 8),)),
    }


def convolve(padded, kernel, height, breadth):
    taps = kernel.reshape(9, kernel.shape[0] // 9, kernel.shape[1])
    total = jnp.zeros((height * breadth, kernel.shape[1]), jnp.float32)
    for tapnum in range(9):
        row_off, col_off = divmod(tapnum, 3)
        piece = padded[row_off:row_off + height, col_off:col_off + breadth].reshape(height * breadth, -1)
        total = total + jnp.dot(piece, taps[tapnum], preferred_element_type=jnp.float32)
    return total.reshape(height, breadth, -1)


def convolve_back(padded, kernel, height, breadth):
    taps = kernel.reshape(9, kernel.shape[0] // 9, kernel.shape[1])
    total = jnp.zeros((height * breadth, kernel.shape[0] // 9), jnp.float32)
    for tapnum in range(9):
        row_off, col_off = divmod(tapnum, 3)
        piece = padded[2 - row_off:2 - row_off + height, 2 - col_off:2 - col_off + breadth].reshape(height * breadth, -1)
        total = total + jnp.dot(piece, taps[tapnum].T, preferred_element_type=jnp.float32)
    return total.reshape(height, breadth, -1)


def kernel_terms(values, padded, height, breadth):
    flat = values.reshape(height * breadth, -1)
    blocks = []
    for tapnum in range(9):
        row_off, col_off = divmod(tapnum, 3)
        piece = padded[2 - row_off:2 - row_off + height, 2 - col_off:2 - col_off + breadth].reshape(height * breadth, -1)
        blocks.append(lax.dot_general(flat, piece, (((0,), (0,)), ((), ())), preferred_element_type=jnp.float32))
    return jnp.concatenate(blocks, axis=0)


def silu_slope(preact):
    sig = jax.nn.sigmoid(preact)
    return sig * (1.0 + preact * (1.0 - sig))


def pad_all(values):
    return jnp.pad(values, ((1, 1), (1, 1), (0, 0)))


def one_section(operands):
    x_in, stored, g_in, first, second = operands
    preact = convolve(pad_all(x_in), first, NROWS, COLS)
    act = jax.nn.silu(preact).astype(jnp.bfloat16)
    forward_out = (x_in.astype(jnp.float32) + convolve(pad_all(act), second, NROWS, COLS)).astype(jnp.bfloat16)
    pre_back = convolve(pad_all(stored), first, NROWS, COLS)
    act_back = jax.nn.silu(pre_back).astype(jnp.bfloat16)
    grad_padded = pad_all(g_in)
    grad_act = convolve_back(grad_padded, second, NROWS, COLS)
    grad_pre = (grad_act * silu_slope(pre_back)).astype(jnp.bfloat16)
    inner_padded = pad_all(grad_pre)
    input_grad = (g_in.astype(jnp.float32) + convolve_back(inner_padded, first, NROWS, COLS)).astype(jnp.bfloat16)
    factor = (NROWS * COLS) ** -0.5
    first_grad = kernel_terms(stored, inner_padded, NROWS, COLS) * factor
    second_grad = kernel_terms(act_back, grad_padded, NROWS, COLS) * factor
    return forward_out, input_grad, first_grad, second_grad


def reference(image, carried, saved, sent_grad, loss_grad, first_kernel, second_kernel):
    inputs = jnp.concatenate([image[None], carried[:-1]], axis=0)
    grads_in = jnp.concatenate([sent_grad[1:], loss_grad[None]], axis=0)
    forward_out, input_grad, first_grad, second_grad = lax.map(one_section, (inputs, saved, grads_in, first_kernel, second_kernel))
    return forward_out, input_grad, first_grad, second_grad
```

```python
import functools
import math

import jax
import jax.numpy as jnp
from jax import lax
from jax.experimental import pallas as pl
from jax.experimental.pallas import tpu as pltpu
from jax.sharding import PartitionSpec as P

MESH = pl.DeviceIdType.MESH
BF16 = jnp.bfloat16
F32 = jnp.float32

H, W, C = 2, 160, 320
M = H * W
CL = 384
PIECE = 90
PR = 96
MAIN = 256
SEND = 5 * PR
NX, NY, NZ = 4, 4, 2


def dot(a, b):
    return jnp.dot(a, b, preferred_element_type=F32)


def dot_t(a, b):
    return lax.dot_general(a, b, (((1,), (1,)), ((), ())), preferred_element_type=F32)


def kernel(
    factor, image, carried, saved, sent_grad, loss_grad, first_hbm, second_hbm,
    fwd_hbm, igrad_hbm, gfirst_hbm, gsecond_hbm,
    first, second, xh, sh, gh, ah, ph, xs, ss, gs, as_, ps, shift_buf, slope, actt,
    terms, send1, recv1, held2, send2, recv2, send3, recv3, keep3, fwd, igrad, gout,
    load_sem, halo_send, halo_recv, s1_sem, r1_sem, s2_sem, r2_sem, s3_sem, r3_sem, out_sem,
):
    sec = lax.axis_index("section")
    band = lax.axis_index("band")
    nsec = lax.axis_size("section")
    nband = lax.axis_size("band")
    y = lax.rem(band, NY)
    z = lax.rem(lax.div(band, NY), NZ)
    x = lax.div(band, NY * NZ)
    next_sec = lax.rem(sec + 1, nsec)
    prev_sec = lax.rem(sec + nsec - 1, nsec)
    up = lax.rem(band + nband - 1, nband)
    down = lax.rem(band + 1, nband)

    def x_peer(d):
        return (sec, (lax.rem(x + d, NX) * NZ + z) * NY + y)

    def y_peer(d):
        return (sec, (x * NZ + z) * NY + lax.rem(y + d, NY))

    z_peer = (sec, (x * NZ + (1 - z)) * NY + y)

    loads = [
        pltpu.make_async_copy(saved, sh.at[pl.ds(1, H)], load_sem.at[0]),
        pltpu.make_async_copy(first_hbm, first, load_sem.at[1]),
        pltpu.make_async_copy(second_hbm, second, load_sem.at[2]),
    ]
    for copy in loads:
        copy.start()

    peers = [(next_sec, band), (next_sec, up), (next_sec, down)]
    peers += [(prev_sec, band), (prev_sec, up), (prev_sec, down)]
    peers += [(sec, up), (sec, down), z_peer]
    peers += [x_peer(d) for d in (1, 2, 3)] + [y_peer(d) for d in (1, 2, 3)]
    barrier = pltpu.get_barrier_semaphore()
    for peer in peers:
        pl.semaphore_signal(barrier, inc=1, device_id=peer, device_id_type=MESH)
    pl.semaphore_wait(barrier, len(peers))

    def remote(src, dst, send_sem, recv_sem, peer):
        return pltpu.make_async_remote_copy(
            src_ref=src, dst_ref=dst, send_sem=send_sem, recv_sem=recv_sem,
            device_id=peer, device_id_type=MESH,
        )

    def halos(src, held, to, k):
        return [
            remote(src.at[H - 1], held.at[0], halo_send.at[k], halo_recv.at[k], (to, down)),
            remote(src.at[0], held.at[H + 1], halo_send.at[k + 1], halo_recv.at[k + 1], (to, up)),
        ]

    def shifted_map(src, held, to, k):
        return halos(src, held, to, k) + [
            remote(src, held.at[pl.ds(1, H)], halo_send.at[k + 2], halo_recv.at[k + 2], (to, band))
        ]

    def start_all(copies):
        for copy in copies:
            copy.start()

    def wait_all(copies):
        for copy in copies:
            copy.wait()

    saved_halo = halos(saved, sh, sec, 0)
    start_all(saved_halo)

    g_copies = shifted_map(sent_grad, gh, prev_sec, 2)

    @pl.when(sec == 0)
    def _():
        start_all(shifted_map(loss_grad, gh, prev_sec, 2))

    @pl.when(sec != 0)
    def _():
        start_all(g_copies)

    x_copies = shifted_map(carried, xh, next_sec, 5)

    @pl.when(sec == nsec - 1)
    def _():
        start_all(shifted_map(image, xh, next_sec, 5))

    @pl.when(sec != nsec - 1)
    def _():
        start_all(x_copies)

    terms[pl.ds(9 * C, 8), :] = jnp.zeros((8, CL), F32)
    terms[:, pl.ds(MAIN, CL - MAIN)] = jnp.zeros((9 * C + 8, CL - MAIN), F32)
    shift_buf[pl.ds(0, 8), :] = jnp.zeros((8, C), F32)
    shift_buf[pl.ds(8 + 4 * W, 8), :] = jnp.zeros((8, C), F32)
    column = lax.broadcasted_iota(jnp.int32, (W, C), 0)

    def build(held, out):
        for r in range(H + 2):
            v = held[r]
            if r == 0:
                v = jnp.where(band == 0, jnp.zeros_like(v), v)
            if r == H + 1:
                v = jnp.where(band == nband - 1, jnp.zeros_like(v), v)
            out[1, pl.ds(r * W, W), :] = v
            shift_buf[pl.ds(8 + r * W, W), :] = v.astype(F32)
        for r in range(H + 2):
            low = shift_buf[pl.ds(7 + r * W, W), :]
            out[0, pl.ds(r * W, W), :] = jnp.where(column == 0, 0.0, low).astype(BF16)
            high = shift_buf[pl.ds(9 + r * W, W), :]
            out[2, pl.ds(r * W, W), :] = jnp.where(column == W - 1, 0.0, high).astype(BF16)

    def conv(maps, weights):
        total = None
        for tap in range(9):
            ky, kx = divmod(tap, 3)
            part = dot(maps[kx, pl.ds(ky * W, M), :], weights[pl.ds(tap * C, C), :])
            total = part if total is None else total + part
        return total

    def conv_t(maps, weights):
        total = None
        for tap in range(9):
            ky, kx = divmod(tap, 3)
            part = dot_t(maps[2 - kx, pl.ds((2 - ky) * W, M), :], weights[pl.ds(tap * C, C), :])
            total = part if total is None else total + part
        return total

    def wgrad(vt, maps):
        for tap in range(9):
            ky, kx = divmod(tap, 3)
            terms[pl.ds(tap * C, C), pl.ds(0, C)] = dot(
                vt[...], maps[2 - kx, pl.ds((2 - ky) * W, M), :]
            )

    lane = lax.broadcasted_iota(jnp.int32, (PR, 128), 1)

    def pack(k):
        for half in range(2):
            for dest in range(4):
                rests = []
                for j in range(4):
                    xx, yy = (dest, j) if half == 0 else (j, dest)
                    row = ((xx * NZ + half) * NY + yy) * PIECE
                    send1[k, half, dest, pl.ds(j * PR, PR), :] = terms[
                        pl.ds(row, PR), pl.ds(0, MAIN)
                    ].astype(BF16)
                    rests.append(terms[pl.ds(row, PR), pl.ds(MAIN, 128)])
                for j in range(2):
                    pair = jnp.where(
                        lane < 64, rests[2 * j], pltpu.roll(rests[2 * j + 1], 64, 1)
                    )
                    send1[k, half, dest, pl.ds(4 * PR, PR), pl.ds(j * 128, 128)] = pair.astype(BF16)

    def stage1(k):
        copies = []
        for d in (1, 3, 2):
            for half, (pos, peer) in enumerate(((x, x_peer), (y, y_peer))):
                copies.append(
                    remote(
                        send1.at[k, half, lax.rem(pos + d, 4)], recv1.at[k, half, d - 1],
                        s1_sem.at[k, half, d - 1], r1_sem.at[k, half, d - 1], peer(d),
                    )
                )
        return copies

    def stage2(k):
        copies = []
        for d in (1, 3, 2):
            for half, (pos, peer) in enumerate(((y, y_peer), (x, x_peer))):
                copies.append(
                    remote(
                        send2.at[k, half, lax.rem(pos + d, 4)], recv2.at[k, half, d - 1],
                        s2_sem.at[k, half, d - 1], r2_sem.at[k, half, d - 1], peer(d),
                    )
                )
        return copies

    def sum1(k):
        for half, pos in enumerate((x, y)):
            def total(rows, lanes):
                value = send1[k, half, pos, rows, lanes].astype(F32)
                for d in range(3):
                    value = value + recv1[k, half, d, rows, lanes].astype(F32)
                return value

            for j in range(4):
                main = total(pl.ds(j * PR, PR), pl.ds(0, MAIN))
                held2[k, half, j, :, pl.ds(0, MAIN)] = main
                send2[k, half, j, :, pl.ds(0, MAIN)] = main.astype(BF16)
            for j in range(2):
                rest = total(pl.ds(4 * PR, PR), pl.ds(j * 128, 128))
                for i, part in enumerate((rest, pltpu.roll(rest, 64, 1))):
                    held2[k, half, 2 * j + i, :, pl.ds(MAIN, 128)] = part
                    send2[k, half, 2 * j + i, :, pl.ds(MAIN, 128)] = part.astype(BF16)

    def sum2(k):
        sums = []
        for half, pos in enumerate((y, x)):
            value = held2[k, half, pos]
            for d in range(3):
                value = value + recv2[k, half, d].astype(F32)
            sums.append(value)
        keep3[k] = jnp.where(z == 0, sums[0], sums[1])
        send3[k] = jnp.where(z == 0, sums[1], sums[0]).astype(BF16)

    def stage3(k):
        return remote(send3.at[k], recv3.at[k], s3_sem.at[k], r3_sem.at[k], z_peer)

    loads[0].wait()
    wait_all(saved_halo)
    build(sh, ss)
    loads[1].wait()
    pre = conv(ss, first)
    sig = jax.nn.sigmoid(pre)
    actt[...] = jnp.transpose(pre * sig).astype(BF16)
    slope[...] = sig * (1.0 + pre * (1.0 - sig))
    wait_all(g_copies)
    build(gh, gs)
    wgrad(actt, gs)
    pack(1)
    second_1 = stage1(1)
    start_all(second_1)

    loads[2].wait()
    grad_pre = (conv_t(gs, second) * slope[...]).astype(BF16)
    for r in range(H):
        ph[1 + r] = grad_pre[r * W : (r + 1) * W]
    pre_halo = halos(ph.at[pl.ds(1, H)], ph, sec, 8)
    start_all(pre_halo)

    wait_all(x_copies)
    build(xh, xs)
    pre = conv(xs, first)
    act = (pre * jax.nn.sigmoid(pre)).astype(BF16)
    for r in range(H):
        ah[1 + r] = act[r * W : (r + 1) * W]
    act_halo = halos(ah.at[pl.ds(1, H)], ah, sec, 10)
    start_all(act_halo)

    wait_all(pre_halo)
    build(ph, ps)
    actt[...] = jnp.transpose(ss[1, pl.ds(W, M), :].astype(F32)).astype(BF16)
    wgrad(actt, ps)
    pack(0)
    first_1 = stage1(0)
    start_all(first_1)

    igrad_flat = conv_t(ps, first)
    for r in range(H):
        igrad[r] = (gh[1 + r].astype(F32) + igrad_flat[r * W : (r + 1) * W]).astype(BF16)
    outs = [pltpu.make_async_copy(igrad, igrad_hbm, out_sem.at[0])]
    outs[0].start()

    wait_all(second_1)
    sum1(1)
    second_2 = stage2(1)
    start_all(second_2)

    wait_all(act_halo)
    build(ah, as_)
    out_flat = conv(as_, second)
    for r in range(H):
        fwd[r] = (xh[1 + r].astype(F32) + out_flat[r * W : (r + 1) * W]).astype(BF16)
    outs.append(pltpu.make_async_copy(fwd, fwd_hbm, out_sem.at[1]))
    outs[1].start()

    wait_all(second_2)
    sum2(1)
    second_3 = stage3(1)
    second_3.start()

    wait_all(first_1)
    sum1(0)
    first_2 = stage2(0)
    start_all(first_2)

    second_3.wait()
    gout[1] = (keep3[1] + recv3[1].astype(F32))[:PIECE, :C] * factor
    outs.append(pltpu.make_async_copy(gout.at[1], gsecond_hbm, out_sem.at[2]))
    outs[2].start()

    wait_all(first_2)
    sum2(0)
    first_3 = stage3(0)
    first_3.start()
    first_3.wait()
    gout[0] = (keep3[0] + recv3[0].astype(F32))[:PIECE, :C] * factor
    outs.append(pltpu.make_async_copy(gout.at[0], gfirst_hbm, out_sem.at[3]))
    outs[3].start()
    for copy in outs:
        copy.wait()


def body(image, carried, saved, sent_grad, loss_grad, first_kernel, second_kernel):
    factor = 1.0 / math.sqrt(H * lax.axis_size("band") * W)
    any_spec = pl.BlockSpec(memory_space=pl.ANY)
    vmem, dma = pltpu.VMEM, pltpu.SemaphoreType.DMA
    halo_map = vmem((H + 2, W, C), BF16)
    moved = vmem((3, (H + 2) * W, C), BF16)
    fwd, igrad, gfirst, gsecond = pl.pallas_call(
        functools.partial(kernel, factor),
        out_shape=(
            jax.ShapeDtypeStruct((H, W, C), BF16),
            jax.ShapeDtypeStruct((H, W, C), BF16),
            jax.ShapeDtypeStruct((PIECE, C), F32),
            jax.ShapeDtypeStruct((PIECE, C), F32),
        ),
        in_specs=[any_spec] * 7,
        out_specs=(any_spec,) * 4,
        scratch_shapes=[
            vmem((9 * C, C), BF16), vmem((9 * C, C), BF16),
            halo_map, halo_map, halo_map, halo_map, halo_map,
            moved, moved, moved, moved, moved,
            vmem((16 + (H + 2) * W, C), F32),
            vmem((M, C), F32),
            vmem((C, M), BF16),
            vmem((9 * C + 8, CL), F32),
            vmem((2, 2, 4, SEND, MAIN), BF16), vmem((2, 2, 3, SEND, MAIN), BF16),
            vmem((2, 2, 4, PR, CL), F32), vmem((2, 2, 4, PR, CL), BF16),
            vmem((2, 2, 3, PR, CL), BF16),
            vmem((2, PR, CL), BF16), vmem((2, PR, CL), BF16), vmem((2, PR, CL), F32),
            vmem((H, W, C), BF16), vmem((H, W, C), BF16),
            vmem((2, PIECE, C), F32),
            dma((3,)), dma((12,)), dma((12,)),
            dma((2, 2, 3)), dma((2, 2, 3)), dma((2, 2, 3)), dma((2, 2, 3)),
            dma((2,)), dma((2,)), dma((4,)),
        ],
        compiler_params=pltpu.CompilerParams(
            collective_id=0, has_side_effects=True, vmem_limit_bytes=56 * 1024 * 1024
        ),
    )(image, carried[0], saved[0], sent_grad[0], loss_grad, first_kernel[0], second_kernel[0])
    return fwd[None], igrad[None], gfirst[None], gsecond[None]


def solution(mesh):
    return jax.shard_map(
        body,
        mesh=mesh,
        in_specs=(
            P("band", None, None),
            P("section", "band", None, None),
            P("section", "band", None, None),
            P("section", "band", None, None),
            P("band", None, None),
            P("section", None, None),
            P("section", None, None),
        ),
        out_specs=(
            P("section", "band", None, None),
            P("section", "band", None, None),
            P("section", "band", None),
            P("section", "band", None),
        ),
        check_vma=False,
    )
```

```python
import functools
import math

import jax
import jax.numpy as jnp
from jax import lax
from jax.experimental import pallas as pl
from jax.experimental.pallas import tpu as pltpu
from jax.sharding import PartitionSpec as P

MESH = pl.DeviceIdType.MESH
BF16 = jnp.bfloat16
F32 = jnp.float32

H, W, C = 2, 160, 320
M = H * W
CL = 384
PIECE = 90
PR = 96
MAIN = 256
SEND = 5 * PR
NX, NY, NZ = 4, 4, 2


def dot(a, b):
    return jnp.dot(a, b, preferred_element_type=F32)


def dot_t(a, b):
    return lax.dot_general(a, b, (((1,), (1,)), ((), ())), preferred_element_type=F32)


def kernel(
    factor, image, carried, saved, sent_grad, loss_grad, first_hbm, second_hbm,
    fwd_hbm, igrad_hbm, gfirst_hbm, gsecond_hbm,
    first_t, second_t, first, second, xh, sh, gh, ah, ph, xs, ss, gs, as_, ps, shift_buf, slope, actt,
    terms, send1, relay, recv1, held2, send2, recv2, send3, recv3, keep3, fwd, igrad, gout,
    load_sem, halo_send, halo_recv, s1_sem, r1_sem, s2_sem, r2_sem, s3_sem, r3_sem, out_sem,
):
    sec = lax.axis_index("section")
    band = lax.axis_index("band")
    nsec = lax.axis_size("section")
    nband = lax.axis_size("band")
    y = lax.rem(band, NY)
    z = lax.rem(lax.div(band, NY), NZ)
    x = lax.div(band, NY * NZ)
    next_sec = lax.rem(sec + 1, nsec)
    prev_sec = lax.rem(sec + nsec - 1, nsec)
    up = lax.rem(band + nband - 1, nband)
    down = lax.rem(band + 1, nband)

    def x_peer(d):
        return (sec, (lax.rem(x + d, NX) * NZ + z) * NY + y)

    def y_peer(d):
        return (sec, (x * NZ + z) * NY + lax.rem(y + d, NY))

    z_peer = (sec, (x * NZ + (1 - z)) * NY + y)

    loads = [
        pltpu.make_async_copy(saved, sh.at[pl.ds(1, H)], load_sem.at[0]),
        pltpu.make_async_copy(first_hbm, first_t, load_sem.at[1]),
        pltpu.make_async_copy(second_hbm, second_t, load_sem.at[2]),
    ]
    for copy in loads:
        copy.start()
    local_g = pltpu.make_async_copy(loss_grad, gh.at[pl.ds(1, H)], load_sem.at[3])
    local_x = pltpu.make_async_copy(image, xh.at[pl.ds(1, H)], load_sem.at[4])

    peers = [(next_sec, band), (next_sec, up), (next_sec, down)]
    peers += [(prev_sec, band), (prev_sec, up), (prev_sec, down)]
    peers += [(sec, up), (sec, down), z_peer]
    peers += [x_peer(d) for d in (1, 2, 3)] + [y_peer(d) for d in (1, 2, 3)]
    barrier = pltpu.get_barrier_semaphore()
    for peer in peers:
        pl.semaphore_signal(barrier, inc=1, device_id=peer, device_id_type=MESH)

    def turn(source, target):
        for k in range(0, 9 * C, 640):
            n = min(640, 9 * C - k)
            target[pl.ds(k, n), :] = jnp.transpose(source[:, pl.ds(k, n)])

    loads[1].wait()
    turn(first_t, first)
    loads[2].wait()
    turn(second_t, second)

    pl.semaphore_wait(barrier, len(peers))

    def remote(src, dst, send_sem, recv_sem, peer):
        return pltpu.make_async_remote_copy(
            src_ref=src, dst_ref=dst, send_sem=send_sem, recv_sem=recv_sem,
            device_id=peer, device_id_type=MESH,
        )

    def halos(src, held, to, k):
        return [
            remote(src.at[H - 1], held.at[0], halo_send.at[k], halo_recv.at[k], (to, down)),
            remote(src.at[0], held.at[H + 1], halo_send.at[k + 1], halo_recv.at[k + 1], (to, up)),
        ]

    def shifted_map(src, held, to, k):
        return halos(src, held, to, k) + [
            remote(src, held.at[pl.ds(1, H)], halo_send.at[k + 2], halo_recv.at[k + 2], (to, band))
        ]

    def start_all(copies):
        for copy in copies:
            copy.start()

    def wait_all(copies):
        for copy in copies:
            copy.wait()

    saved_halo = halos(saved, sh, sec, 0)
    start_all(saved_halo)

    def start_map(src, edge_src, local, held, to, k, edge):
        @pl.when(sec == edge)
        def _():
            start_all(halos(edge_src, held, sec, k + 3))
            local.start()

        @pl.when(sec != nsec - 1 - edge)
        def _():
            start_all(shifted_map(src, held, to, k))

    def wait_map(src, edge_src, local, held, to, k, edge):
        copies = shifted_map(src, held, to, k)

        @pl.when(sec != nsec - 1 - edge)
        def _():
            for copy in copies:
                copy.wait_send()

        @pl.when(sec == edge)
        def _():
            edges = halos(edge_src, held, sec, k + 3)
            for copy in edges:
                copy.wait_send()
                copy.wait_recv()
            local.wait()

        @pl.when(sec != edge)
        def _():
            for copy in copies:
                copy.wait_recv()

    g_map = (sent_grad, loss_grad, local_g, gh, prev_sec, 2, nsec - 1)
    x_map = (carried, image, local_x, xh, next_sec, 7, 0)
    start_map(*g_map)

    terms[pl.ds(9 * C, 8), :] = jnp.zeros((8, CL), F32)
    terms[:, pl.ds(MAIN, CL - MAIN)] = jnp.zeros((9 * C + 8, CL - MAIN), F32)
    shift_buf[pl.ds(0, 8), :] = jnp.zeros((8, C), F32)
    shift_buf[pl.ds(8 + 4 * W, 8), :] = jnp.zeros((8, C), F32)
    column = lax.broadcasted_iota(jnp.int32, (W, C), 0)

    def build(held, out):
        for r in range(H + 2):
            v = held[r]
            if r == 0:
                v = jnp.where(band == 0, jnp.zeros_like(v), v)
            if r == H + 1:
                v = jnp.where(band == nband - 1, jnp.zeros_like(v), v)
            out[1, pl.ds(r * W, W), :] = v
            shift_buf[pl.ds(8 + r * W, W), :] = v.astype(F32)
        for r in range(H + 2):
            low = shift_buf[pl.ds(7 + r * W, W), :]
            out[0, pl.ds(r * W, W), :] = jnp.where(column == 0, 0.0, low).astype(BF16)
            high = shift_buf[pl.ds(9 + r * W, W), :]
            out[2, pl.ds(r * W, W), :] = jnp.where(column == W - 1, 0.0, high).astype(BF16)

    def conv(maps, weights):
        total = None
        for tap in range(9):
            ky, kx = divmod(tap, 3)
            part = dot(maps[kx, pl.ds(ky * W, M), :], weights[pl.ds(tap * C, C), :])
            total = part if total is None else total + part
        return total

    def conv_t(maps, weights):
        total = None
        for tap in range(9):
            ky, kx = divmod(tap, 3)
            part = dot_t(maps[2 - kx, pl.ds((2 - ky) * W, M), :], weights[pl.ds(tap * C, C), :])
            total = part if total is None else total + part
        return total

    def wgrad(vt, maps):
        for tap in range(9):
            ky, kx = divmod(tap, 3)
            terms[pl.ds(tap * C, C), pl.ds(0, C)] = dot(
                vt[...], maps[2 - kx, pl.ds((2 - ky) * W, M), :]
            )

    lane = lax.broadcasted_iota(jnp.int32, (PR, 128), 1)

    def pack(k):
        for half in range(2):
            for dest in range(4):
                rests = []
                for j in range(4):
                    xx, yy = (dest, j) if half == 0 else (j, dest)
                    row = ((xx * NZ + half) * NY + yy) * PIECE
                    send1[k, half, dest, pl.ds(j * PR, PR), :] = terms[
                        pl.ds(row, PR), pl.ds(0, MAIN)
                    ].astype(BF16)
                    rests.append(terms[pl.ds(row, PR), pl.ds(MAIN, 128)])
                for j in range(2):
                    pair = jnp.where(
                        lane < 64, rests[2 * j], pltpu.roll(rests[2 * j + 1], 64, 1)
                    )
                    send1[k, half, dest, pl.ds(4 * PR, PR), pl.ds(j * 128, 128)] = pair.astype(BF16)

    low, high = pl.ds(0, SEND // 2), pl.ds(SEND // 2, SEND // 2)

    def stage1(k):
        relays, plain, added = [], [], []
        for half, (pos, peer) in enumerate(((x, x_peer), (y, y_peer))):
            for side, (d, via, own) in enumerate(((1, low, high), (3, high, low))):
                def copy(ahead, rows, dst, i):
                    return remote(
                        send1.at[k, half, lax.rem(pos + ahead, 4), rows], dst,
                        s1_sem.at[k, half, i + side], r1_sem.at[k, half, i + side], peer(d),
                    )

                relays.append(copy(2, via, relay.at[k, half, side], 0))
                plain.append(copy(d, own, recv1.at[k, half, side, own], 2))
                added.append(copy(d, via, recv1.at[k, half, side, via], 4))
        return relays, plain, added

    def add_relays(k):
        for half, pos in enumerate((x, y)):
            for side, (d, via) in enumerate(((1, low), (3, high))):
                ahead = lax.rem(pos + d, 4)
                send1[k, half, ahead, via, :] = (
                    send1[k, half, ahead, via, :].astype(F32) + relay[k, half, side].astype(F32)
                ).astype(BF16)

    def stage2(k):
        copies = []
        for d in (1, 3, 2):
            for half, (pos, peer) in enumerate(((y, y_peer), (x, x_peer))):
                copies.append(
                    remote(
                        send2.at[k, half, lax.rem(pos + d, 4)], recv2.at[k, half, d - 1],
                        s2_sem.at[k, half, d - 1], r2_sem.at[k, half, d - 1], peer(d),
                    )
                )
        return copies

    def sum1(k):
        for half, pos in enumerate((x, y)):
            def total(rows, lanes):
                value = send1[k, half, pos, rows, lanes].astype(F32)
                for d in range(2):
                    value = value + recv1[k, half, d, rows, lanes].astype(F32)
                return value

            for j in range(4):
                main = total(pl.ds(j * PR, PR), pl.ds(0, MAIN))
                held2[k, half, j, :, pl.ds(0, MAIN)] = main
                send2[k, half, j, :, pl.ds(0, MAIN)] = main.astype(BF16)
            for j in range(2):
                rest = total(pl.ds(4 * PR, PR), pl.ds(j * 128, 128))
                for i, part in enumerate((rest, pltpu.roll(rest, 64, 1))):
                    held2[k, half, 2 * j + i, :, pl.ds(MAIN, 128)] = part
                    send2[k, half, 2 * j + i, :, pl.ds(MAIN, 128)] = part.astype(BF16)

    def sum2(k):
        sums = []
        for half, pos in enumerate((y, x)):
            value = held2[k, half, pos]
            for d in range(3):
                value = value + recv2[k, half, d].astype(F32)
            sums.append(value)
        keep3[k] = jnp.where(z == 0, sums[0], sums[1])
        send3[k] = jnp.where(z == 0, sums[1], sums[0]).astype(BF16)

    def stage3(k):
        return remote(send3.at[k], recv3.at[k], s3_sem.at[k], r3_sem.at[k], z_peer)

    loads[0].wait()
    wait_all(saved_halo)
    build(sh, ss)
    pre = conv(ss, first)
    sig = jax.nn.sigmoid(pre)
    actt[...] = jnp.transpose(pre * sig).astype(BF16)
    slope[...] = sig * (1.0 + pre * (1.0 - sig))
    wait_map(*g_map)
    start_map(*x_map)
    build(gh, gs)
    wgrad(actt, gs)
    pack(1)
    second_relays, second_plain, second_added = stage1(1)
    start_all(second_relays + second_plain)

    grad_pre = (conv_t(gs, second) * slope[...]).astype(BF16)
    for r in range(H):
        ph[1 + r] = grad_pre[r * W : (r + 1) * W]
    pre_halo = halos(ph.at[pl.ds(1, H)], ph, sec, 12)
    start_all(pre_halo)

    for tap in range(9):
        ky, kx = divmod(tap, 3)
        terms[pl.ds(tap * C, C), pl.ds(0, C)] = dot(
            jnp.transpose(ss[kx, pl.ds(ky * W, M), :]), grad_pre
        )
    wait_all(second_relays)
    add_relays(1)
    start_all(second_added)
    pack(0)
    first_relays, first_plain, first_added = stage1(0)
    start_all(first_relays + first_plain)

    wait_map(*x_map)
    build(xh, xs)
    pre = conv(xs, first)
    act = (pre * jax.nn.sigmoid(pre)).astype(BF16)
    for r in range(H):
        ah[1 + r] = act[r * W : (r + 1) * W]
    act_halo = halos(ah.at[pl.ds(1, H)], ah, sec, 14)
    start_all(act_halo)

    wait_all(first_relays)
    add_relays(0)
    start_all(first_added)

    wait_all(second_plain + second_added)
    sum1(1)
    second_2 = stage2(1)
    start_all(second_2)

    wait_all(pre_halo)
    build(ph, ps)
    igrad_flat = conv_t(ps, first)
    for r in range(H):
        igrad[r] = (gh[1 + r].astype(F32) + igrad_flat[r * W : (r + 1) * W]).astype(BF16)
    outs = [pltpu.make_async_copy(igrad, igrad_hbm, out_sem.at[0])]
    outs[0].start()

    wait_all(first_plain + first_added)
    sum1(0)
    first_2 = stage2(0)
    start_all(first_2)

    wait_all(second_2)
    sum2(1)
    second_3 = stage3(1)
    second_3.start()

    wait_all(first_2)
    sum2(0)
    first_3 = stage3(0)
    first_3.start()

    wait_all(act_halo)
    build(ah, as_)
    out_flat = conv(as_, second)
    for r in range(H):
        fwd[r] = (xh[1 + r].astype(F32) + out_flat[r * W : (r + 1) * W]).astype(BF16)
    outs.append(pltpu.make_async_copy(fwd, fwd_hbm, out_sem.at[1]))
    outs[1].start()

    for k, copy, out in ((1, second_3, gsecond_hbm), (0, first_3, gfirst_hbm)):
        copy.wait()
        gout[k] = (keep3[k] + recv3[k].astype(F32))[:PIECE, :C] * factor
        outs.append(pltpu.make_async_copy(gout.at[k], out, out_sem.at[3 - k]))
        outs[-1].start()
    for copy in outs:
        copy.wait()


def copy_out(fwd, igrad, gfirst, gsecond, fwd_out, igrad_out, gfirst_out, gsecond_out):
    fwd_out[...] = fwd[...]
    igrad_out[...] = igrad[...]
    gfirst_out[...] = gfirst[...].reshape(PIECE, 1, C)
    gsecond_out[...] = gsecond[...].reshape(PIECE, 1, C)


def body(image, carried, saved, sent_grad, loss_grad, first_kernel, second_kernel):
    factor = 1.0 / math.sqrt(H * lax.axis_size("band") * W)
    any_spec = pl.BlockSpec(memory_space=pl.ANY)
    vmem, dma = pltpu.VMEM, pltpu.SemaphoreType.DMA
    halo_map = vmem((H + 2, W, C), BF16)
    moved = vmem((3, (H + 2) * W, C), BF16)
    fwd, igrad, gfirst, gsecond = pl.pallas_call(
        functools.partial(kernel, factor),
        out_shape=(
            jax.ShapeDtypeStruct((H, W, C), BF16),
            jax.ShapeDtypeStruct((H, W, C), BF16),
            jax.ShapeDtypeStruct((PIECE, C), F32),
            jax.ShapeDtypeStruct((PIECE, C), F32),
        ),
        in_specs=[any_spec] * 7,
        out_specs=(any_spec,) * 4,
        scratch_shapes=[
            vmem((C, 9 * C), BF16), vmem((C, 9 * C), BF16),
            vmem((9 * C, C), BF16), vmem((9 * C, C), BF16),
            halo_map, halo_map, halo_map, halo_map, halo_map,
            moved, moved, moved, moved, moved,
            vmem((16 + (H + 2) * W, C), F32),
            vmem((M, C), F32),
            vmem((C, M), BF16),
            vmem((9 * C + 8, CL), F32),
            vmem((2, 2, 4, SEND, MAIN), BF16), vmem((2, 2, 2, SEND // 2, MAIN), BF16),
            vmem((2, 2, 2, SEND, MAIN), BF16),
            vmem((2, 2, 4, PR, CL), F32), vmem((2, 2, 4, PR, CL), BF16),
            vmem((2, 2, 3, PR, CL), BF16),
            vmem((2, PR, CL), BF16), vmem((2, PR, CL), BF16), vmem((2, PR, CL), F32),
            vmem((H, W, C), BF16), vmem((H, W, C), BF16),
            vmem((2, PIECE, C), F32),
            dma((5,)), dma((16,)), dma((16,)),
            dma((2, 2, 6)), dma((2, 2, 6)), dma((2, 2, 3)), dma((2, 2, 3)),
            dma((2,)), dma((2,)), dma((4,)),
        ],
        compiler_params=pltpu.CompilerParams(
            collective_id=0, has_side_effects=True, vmem_limit_bytes=56 * 1024 * 1024
        ),
    )(image, carried[0], saved[0], sent_grad[0], loss_grad, first_kernel[0].T, second_kernel[0].T)
    vmem_spec = pl.BlockSpec(memory_space=pltpu.VMEM)
    grad_shape = jax.ShapeDtypeStruct((PIECE, 1, C), F32)
    fwd, igrad, gfirst, gsecond = pl.pallas_call(
        copy_out,
        out_shape=(fwd, igrad, grad_shape, grad_shape),
        in_specs=[vmem_spec] * 4,
        out_specs=(vmem_spec,) * 4,
    )(fwd, igrad, gfirst, gsecond)
    return fwd[None], igrad[None], gfirst.reshape(1, PIECE, C), gsecond.reshape(1, PIECE, C)


def solution(mesh):
    return jax.shard_map(
        body,
        mesh=mesh,
        in_specs=(
            P("band", None, None),
            P("section", "band", None, None),
            P("section", "band", None, None),
            P("section", "band", None, None),
            P("band", None, None),
            P("section", None, None),
            P("section", None, None),
        ),
        out_specs=(
            P("section", "band", None, None),
            P("section", "band", None, None),
            P("section", "band", None),
            P("section", "band", None),
        ),
        check_vma=False,
    )
```

```python
import functools
import math

import jax
import jax.numpy as jnp
from jax import lax
from jax.experimental import pallas as pl
from jax.experimental.pallas import tpu as pltpu
from jax.sharding import PartitionSpec as P

MESH = pl.DeviceIdType.MESH
BF16 = jnp.bfloat16
F32 = jnp.float32

H, W, C = 2, 160, 320
M = H * W
CL = 384
PIECE = 90
PR = 96
MAIN = 256
SEND = 5 * PR
Q = W // 4
ROW = W + Q
NX, NY, NZ = 4, 4, 2


def dot(a, b):
    return jnp.dot(a, b, preferred_element_type=F32)


def dot_t(a, b):
    return lax.dot_general(a, b, (((1,), (1,)), ((), ())), preferred_element_type=F32)


def kernel(
    factor, image, carried, saved, sent_grad, loss_grad, first_hbm, second_hbm,
    fwd_hbm, igrad_hbm, gfirst_hbm, gsecond_hbm,
    first_t, second_t, first, second, raw, gsend, xsend, xh, sh, gh, ah, ph, xs, ss, gs, as_, ps, shift_buf, slope, actt,
    terms, send1, relay, recv1, held2, send2, recv2, send3, recv3, keep3, fwd, igrad, gout,
    load_sem, halo_send, halo_recv, s1_sem, r1_sem, s2_sem, r2_sem, s3_sem, r3_sem, out_sem,
):
    sec = lax.axis_index("section")
    band = lax.axis_index("band")
    nsec = lax.axis_size("section")
    nband = lax.axis_size("band")
    y = lax.rem(band, NY)
    z = lax.rem(lax.div(band, NY), NZ)
    x = lax.div(band, NY * NZ)
    next_sec = lax.rem(sec + 1, nsec)
    prev_sec = lax.rem(sec + nsec - 1, nsec)
    up = lax.rem(band + nband - 1, nband)
    down = lax.rem(band + 1, nband)

    def x_peer(d):
        return (sec, (lax.rem(x + d, NX) * NZ + z) * NY + y)

    def y_peer(d):
        return (sec, (x * NZ + z) * NY + lax.rem(y + d, NY))

    z_peer = (sec, (x * NZ + (1 - z)) * NY + y)

    loads = [
        pltpu.make_async_copy(value, raw.at[i], load_sem.at[i])
        for i, value in enumerate((saved, sent_grad, carried, loss_grad, image))
    ]
    loads += [
        pltpu.make_async_copy(first_hbm, first_t, load_sem.at[5]),
        pltpu.make_async_copy(second_hbm, second_t, load_sem.at[6]),
    ]
    for copy in loads:
        copy.start()

    peers = [(next_sec, band), (next_sec, up), (next_sec, down)]
    peers += [(prev_sec, band), (prev_sec, up), (prev_sec, down)]
    peers += [(sec, up), (sec, down), z_peer]
    peers += [x_peer(d) for d in (1, 2, 3)] + [y_peer(d) for d in (1, 2, 3)]
    barrier = pltpu.get_barrier_semaphore()
    for peer in peers:
        pl.semaphore_signal(barrier, inc=1, device_id=peer, device_id_type=MESH)

    def pack_map(i, target, start):
        for r in range(H):
            target[start + r, pl.ds(0, W), :] = raw[i, r, :, pl.ds(0, MAIN)]
            rest = raw[i, r, :, pl.ds(MAIN, C - MAIN)].astype(F32)
            for j in range(2):
                one, two = rest[2 * j * Q : (2 * j + 1) * Q], rest[(2 * j + 1) * Q : (2 * j + 2) * Q]
                pair = jnp.concatenate([one, two], axis=1)
                target[start + r, pl.ds(W, Q), pl.ds(128 * j, 128)] = pair.astype(BF16)

    loads[0].wait()
    pack_map(0, sh, 1)
    loads[1].wait()
    pack_map(1, gsend, 0)
    loads[2].wait()
    pack_map(2, xsend, 0)
    loads[3].wait()
    loads[4].wait()

    @pl.when(sec == nsec - 1)
    def _():
        pack_map(3, gh, 1)

    @pl.when(sec == 0)
    def _():
        pack_map(4, xh, 1)

    pl.semaphore_wait(barrier, len(peers))

    def remote(src, dst, send_sem, recv_sem, peer):
        return pltpu.make_async_remote_copy(
            src_ref=src, dst_ref=dst, send_sem=send_sem, recv_sem=recv_sem,
            device_id=peer, device_id_type=MESH,
        )

    def halos(src, held, to, k):
        return [
            remote(src.at[H - 1], held.at[0], halo_send.at[k], halo_recv.at[k], (to, down)),
            remote(src.at[0], held.at[H + 1], halo_send.at[k + 1], halo_recv.at[k + 1], (to, up)),
        ]

    def shifted_map(src, held, to, k):
        return halos(src, held, to, k) + [
            remote(src, held.at[pl.ds(1, H)], halo_send.at[k + 2], halo_recv.at[k + 2], (to, band))
        ]

    def start_all(copies):
        for copy in copies:
            copy.start()

    def wait_all(copies):
        for copy in copies:
            copy.wait()

    saved_halo = halos(sh.at[pl.ds(1, H)], sh, sec, 0)
    start_all(saved_halo)

    def start_map(src, held, to, k, edge):
        @pl.when(sec == edge)
        def _():
            start_all(halos(held.at[pl.ds(1, H)], held, sec, k + 3))

        @pl.when(sec != nsec - 1 - edge)
        def _():
            start_all(shifted_map(src, held, to, k))

    def wait_map(src, held, to, k, edge):
        copies = shifted_map(src, held, to, k)

        @pl.when(sec != nsec - 1 - edge)
        def _():
            for copy in copies:
                copy.wait_send()

        @pl.when(sec == edge)
        def _():
            wait_all(halos(held.at[pl.ds(1, H)], held, sec, k + 3))

        @pl.when(sec != edge)
        def _():
            for copy in copies:
                copy.wait_recv()

    g_map = (gsend, gh, prev_sec, 2, nsec - 1)
    x_map = (xsend, xh, next_sec, 7, 0)
    start_map(*g_map)

    def turn(source, target):
        for k in range(0, 9 * C, 640):
            n = min(640, 9 * C - k)
            target[pl.ds(k, n), :] = jnp.transpose(source[:, pl.ds(k, n)])

    loads[5].wait()
    turn(first_t, first)
    loads[6].wait()
    turn(second_t, second)

    terms[pl.ds(9 * C, 8), :] = jnp.zeros((8, CL), F32)
    terms[:, pl.ds(MAIN, CL - MAIN)] = jnp.zeros((9 * C + 8, CL - MAIN), F32)
    shift_buf[pl.ds(0, 8), :] = jnp.zeros((8, CL), F32)
    shift_buf[pl.ds(8 + 4 * W, 8), :] = jnp.zeros((8, CL), F32)
    column = lax.broadcasted_iota(jnp.int32, (W, C), 0)

    def build(held, out):
        for r in range(H + 2):
            main = held[r, pl.ds(0, W), :]
            pairs = [held[r, pl.ds(W, Q), pl.ds(128 * j, 128)].astype(F32) for j in range(2)]
            rest = jnp.concatenate(
                [part for pair in pairs for part in (pair, pltpu.roll(pair, 64, 1))], axis=0
            )
            outside = None
            if r == 0:
                outside = band == 0
            if r == H + 1:
                outside = band == nband - 1
            if outside is not None:
                main = jnp.where(outside, jnp.zeros_like(main), main)
                rest = jnp.where(outside, jnp.zeros_like(rest), rest)
            rows = pl.ds(8 + r * W, W)
            shift_buf[rows, pl.ds(0, MAIN)] = main.astype(F32)
            shift_buf[rows, pl.ds(MAIN, 128)] = rest
            out[1, pl.ds(r * W, W), :] = shift_buf[rows, pl.ds(0, C)].astype(BF16)
        for r in range(H + 2):
            low = shift_buf[pl.ds(7 + r * W, W), pl.ds(0, C)]
            out[0, pl.ds(r * W, W), :] = jnp.where(column == 0, 0.0, low).astype(BF16)
            high = shift_buf[pl.ds(9 + r * W, W), pl.ds(0, C)]
            out[2, pl.ds(r * W, W), :] = jnp.where(column == W - 1, 0.0, high).astype(BF16)

    def conv(maps, weights):
        total = None
        for tap in range(9):
            ky, kx = divmod(tap, 3)
            part = dot(maps[kx, pl.ds(ky * W, M), :], weights[pl.ds(tap * C, C), :])
            total = part if total is None else total + part
        return total

    def conv_t(maps, weights):
        total = None
        for tap in range(9):
            ky, kx = divmod(tap, 3)
            part = dot_t(maps[2 - kx, pl.ds((2 - ky) * W, M), :], weights[pl.ds(tap * C, C), :])
            total = part if total is None else total + part
        return total

    def wgrad(vt, maps):
        for tap in range(9):
            ky, kx = divmod(tap, 3)
            terms[pl.ds(tap * C, C), pl.ds(0, C)] = dot(
                vt[...], maps[2 - kx, pl.ds((2 - ky) * W, M), :]
            )

    lane = lax.broadcasted_iota(jnp.int32, (PR, 128), 1)

    def pack(k):
        for half in range(2):
            for dest in range(4):
                rests = []
                for j in range(4):
                    xx, yy = (dest, j) if half == 0 else (j, dest)
                    row = ((xx * NZ + half) * NY + yy) * PIECE
                    send1[k, half, dest, pl.ds(j * PR, PR), :] = terms[
                        pl.ds(row, PR), pl.ds(0, MAIN)
                    ].astype(BF16)
                    rests.append(terms[pl.ds(row, PR), pl.ds(MAIN, 128)])
                for j in range(2):
                    pair = jnp.where(
                        lane < 64, rests[2 * j], pltpu.roll(rests[2 * j + 1], 64, 1)
                    )
                    send1[k, half, dest, pl.ds(4 * PR, PR), pl.ds(j * 128, 128)] = pair.astype(BF16)

    low, high = pl.ds(0, SEND // 2), pl.ds(SEND // 2, SEND // 2)

    def stage1(k):
        relays, plain, added = [], [], []
        for half, (pos, peer) in enumerate(((x, x_peer), (y, y_peer))):
            for side, (d, via, own) in enumerate(((1, low, high), (3, high, low))):
                def copy(ahead, rows, dst, i):
                    return remote(
                        send1.at[k, half, lax.rem(pos + ahead, 4), rows], dst,
                        s1_sem.at[k, half, i + side], r1_sem.at[k, half, i + side], peer(d),
                    )

                relays.append(copy(2, via, relay.at[k, half, side], 0))
                plain.append(copy(d, own, recv1.at[k, half, side, own], 2))
                added.append(copy(d, via, recv1.at[k, half, side, via], 4))
        return relays, plain, added

    def add_relays(k):
        for half, pos in enumerate((x, y)):
            for side, (d, via) in enumerate(((1, low), (3, high))):
                ahead = lax.rem(pos + d, 4)
                send1[k, half, ahead, via, :] = (
                    send1[k, half, ahead, via, :].astype(F32) + relay[k, half, side].astype(F32)
                ).astype(BF16)

    def stage2(k):
        copies = []
        for d in (1, 3, 2):
            for half, (pos, peer) in enumerate(((y, y_peer), (x, x_peer))):
                copies.append(
                    remote(
                        send2.at[k, half, lax.rem(pos + d, 4)], recv2.at[k, half, d - 1],
                        s2_sem.at[k, half, d - 1], r2_sem.at[k, half, d - 1], peer(d),
                    )
                )
        return copies

    def sum1(k):
        for half, pos in enumerate((x, y)):
            def total(rows, lanes):
                value = send1[k, half, pos, rows, lanes].astype(F32)
                for d in range(2):
                    value = value + recv1[k, half, d, rows, lanes].astype(F32)
                return value

            for j in range(4):
                main = total(pl.ds(j * PR, PR), pl.ds(0, MAIN))
                held2[k, half, j, :, pl.ds(0, MAIN)] = main
                send2[k, half, j, :, pl.ds(0, MAIN)] = main.astype(BF16)
            for j in range(2):
                rest = total(pl.ds(4 * PR, PR), pl.ds(j * 128, 128))
                for i, part in enumerate((rest, pltpu.roll(rest, 64, 1))):
                    held2[k, half, 2 * j + i, :, pl.ds(MAIN, 128)] = part
                    send2[k, half, 2 * j + i, :, pl.ds(MAIN, 128)] = part.astype(BF16)

    def sum2(k):
        sums = []
        for half, pos in enumerate((y, x)):
            value = held2[k, half, pos]
            for d in range(3):
                value = value + recv2[k, half, d].astype(F32)
            sums.append(value)
        keep3[k] = jnp.where(z == 0, sums[0], sums[1])
        send3[k] = jnp.where(z == 0, sums[1], sums[0]).astype(BF16)

    def stage3(k):
        return remote(send3.at[k], recv3.at[k], s3_sem.at[k], r3_sem.at[k], z_peer)

    wait_all(saved_halo)
    build(sh, ss)
    pre = conv(ss, first)
    sig = jax.nn.sigmoid(pre)
    actt[...] = jnp.transpose(pre * sig).astype(BF16)
    slope[...] = sig * (1.0 + pre * (1.0 - sig))
    wait_map(*g_map)
    start_map(*x_map)
    build(gh, gs)
    wgrad(actt, gs)
    pack(1)
    second_relays, second_plain, second_added = stage1(1)
    start_all(second_relays + second_plain)

    grad_pre = (conv_t(gs, second) * slope[...]).astype(BF16)
    for r in range(H):
        raw[0, r] = grad_pre[r * W : (r + 1) * W]
    pack_map(0, ph, 1)
    pre_halo = halos(ph.at[pl.ds(1, H)], ph, sec, 12)
    start_all(pre_halo)

    for tap in range(9):
        ky, kx = divmod(tap, 3)
        terms[pl.ds(tap * C, C), pl.ds(0, C)] = dot(
            jnp.transpose(ss[kx, pl.ds(ky * W, M), :]), grad_pre
        )
    wait_all(second_relays)
    add_relays(1)
    start_all(second_added)
    pack(0)
    first_relays, first_plain, first_added = stage1(0)
    start_all(first_relays + first_plain)

    wait_all(first_relays)
    add_relays(0)
    start_all(first_added)

    wait_all(second_plain + second_added)
    sum1(1)
    second_2 = stage2(1)
    start_all(second_2)

    wait_map(*x_map)
    build(xh, xs)
    pre = conv(xs, first)
    act = (pre * jax.nn.sigmoid(pre)).astype(BF16)
    for r in range(H):
        raw[1, r] = act[r * W : (r + 1) * W]
    pack_map(1, ah, 1)
    act_halo = halos(ah.at[pl.ds(1, H)], ah, sec, 14)
    start_all(act_halo)

    wait_all(first_plain + first_added)
    sum1(0)
    first_2 = stage2(0)
    start_all(first_2)

    wait_all(pre_halo)
    build(ph, ps)
    igrad_flat = conv_t(ps, first)
    for r in range(H):
        igrad[r] = (gs[1, pl.ds((1 + r) * W, W), :].astype(F32) + igrad_flat[r * W : (r + 1) * W]).astype(BF16)
    outs = [pltpu.make_async_copy(igrad, igrad_hbm, out_sem.at[0])]
    outs[0].start()

    wait_all(second_2)
    sum2(1)
    second_3 = stage3(1)
    second_3.start()

    wait_all(first_2)
    sum2(0)
    first_3 = stage3(0)
    first_3.start()

    wait_all(act_halo)
    build(ah, as_)
    out_flat = conv(as_, second)
    for r in range(H):
        fwd[r] = (xs[1, pl.ds((1 + r) * W, W), :].astype(F32) + out_flat[r * W : (r + 1) * W]).astype(BF16)
    outs.append(pltpu.make_async_copy(fwd, fwd_hbm, out_sem.at[1]))
    outs[1].start()

    for k, copy, out in ((1, second_3, gsecond_hbm), (0, first_3, gfirst_hbm)):
        copy.wait()
        gout[k] = (keep3[k] + recv3[k].astype(F32))[:PIECE, :C] * factor
        outs.append(pltpu.make_async_copy(gout.at[k], out, out_sem.at[3 - k]))
        outs[-1].start()
    for copy in outs:
        copy.wait()


def copy_out(fwd, igrad, gfirst, gsecond, fwd_out, igrad_out, gfirst_out, gsecond_out):
    fwd_out[...] = fwd[...]
    igrad_out[...] = igrad[...]
    gfirst_out[...] = gfirst[...].reshape(PIECE, 1, C)
    gsecond_out[...] = gsecond[...].reshape(PIECE, 1, C)


def body(image, carried, saved, sent_grad, loss_grad, first_kernel, second_kernel):
    factor = 1.0 / math.sqrt(H * lax.axis_size("band") * W)
    any_spec = pl.BlockSpec(memory_space=pl.ANY)
    vmem, dma = pltpu.VMEM, pltpu.SemaphoreType.DMA
    halo_map = vmem((H + 2, ROW, MAIN), BF16)
    moved = vmem((3, (H + 2) * W, C), BF16)
    fwd, igrad, gfirst, gsecond = pl.pallas_call(
        functools.partial(kernel, factor),
        out_shape=(
            jax.ShapeDtypeStruct((H, W, C), BF16),
            jax.ShapeDtypeStruct((H, W, C), BF16),
            jax.ShapeDtypeStruct((PIECE, C), F32),
            jax.ShapeDtypeStruct((PIECE, C), F32),
        ),
        in_specs=[any_spec] * 7,
        out_specs=(any_spec,) * 4,
        scratch_shapes=[
            vmem((C, 9 * C), BF16), vmem((C, 9 * C), BF16),
            vmem((9 * C, C), BF16), vmem((9 * C, C), BF16),
            vmem((5, H, W, C), BF16), vmem((H, ROW, MAIN), BF16), vmem((H, ROW, MAIN), BF16),
            halo_map, halo_map, halo_map, halo_map, halo_map,
            moved, moved, moved, moved, moved,
            vmem((16 + (H + 2) * W, CL), F32),
            vmem((M, C), F32),
            vmem((C, M), BF16),
            vmem((9 * C + 8, CL), F32),
            vmem((2, 2, 4, SEND, MAIN), BF16), vmem((2, 2, 2, SEND // 2, MAIN), BF16),
            vmem((2, 2, 2, SEND, MAIN), BF16),
            vmem((2, 2, 4, PR, CL), F32), vmem((2, 2, 4, PR, CL), BF16),
            vmem((2, 2, 3, PR, CL), BF16),
            vmem((2, PR, CL), BF16), vmem((2, PR, CL), BF16), vmem((2, PR, CL), F32),
            vmem((H, W, C), BF16), vmem((H, W, C), BF16),
            vmem((2, PIECE, C), F32),
            dma((7,)), dma((16,)), dma((16,)),
            dma((2, 2, 6)), dma((2, 2, 6)), dma((2, 2, 3)), dma((2, 2, 3)),
            dma((2,)), dma((2,)), dma((4,)),
        ],
        compiler_params=pltpu.CompilerParams(
            collective_id=0, has_side_effects=True, vmem_limit_bytes=56 * 1024 * 1024
        ),
    )(image, carried[0], saved[0], sent_grad[0], loss_grad, first_kernel[0].T, second_kernel[0].T)
    vmem_spec = pl.BlockSpec(memory_space=pltpu.VMEM)
    grad_shape = jax.ShapeDtypeStruct((PIECE, 1, C), F32)
    fwd, igrad, gfirst, gsecond = pl.pallas_call(
        copy_out,
        out_shape=(fwd, igrad, grad_shape, grad_shape),
        in_specs=[vmem_spec] * 4,
        out_specs=(vmem_spec,) * 4,
    )(fwd, igrad, gfirst, gsecond)
    return fwd[None], igrad[None], gfirst.reshape(1, PIECE, C), gsecond.reshape(1, PIECE, C)


def solution(mesh):
    return jax.shard_map(
        body,
        mesh=mesh,
        in_specs=(
            P("band", None, None),
            P("section", "band", None, None),
            P("section", "band", None, None),
            P("section", "band", None, None),
            P("band", None, None),
            P("section", None, None),
            P("section", None, None),
        ),
        out_specs=(
            P("section", "band", None, None),
            P("section", "band", None, None),
            P("section", "band", None),
            P("section", "band", None),
        ),
        check_vma=False,
    )
```

```python
import functools
import math

import jax
import jax.numpy as jnp
from jax import lax
from jax.experimental import pallas as pl
from jax.experimental.pallas import tpu as pltpu
from jax.sharding import PartitionSpec as P

MESH = pl.DeviceIdType.MESH
BF16 = jnp.bfloat16
F32 = jnp.float32

H, W, C = 2, 160, 320
M = H * W
CL = 384
PIECE = 90
PR = 96
MAIN = 256
SEND = 5 * PR
Q = W // 4
ROW = W + Q
NX, NY, NZ = 4, 4, 2


def dot(a, b):
    return jnp.dot(a, b, preferred_element_type=F32)


def dot_t(a, b):
    return lax.dot_general(a, b, (((1,), (1,)), ((), ())), preferred_element_type=F32)


def kernel(
    factor, image, carried, saved, sent_grad, loss_grad, first_hbm, second_hbm,
    fwd, igrad, gfirst, gsecond,
    first_t, second_t, first, second, raw, gsend, xsend, xh, sh, gh, ah, ph, xs, ss, gs, as_, ps, shift_buf, slope, actt,
    terms, send1, relay, recv1, held2, send2, recv2, send3, recv3, keep3,
    load_sem, halo_send, halo_recv, s1_sem, r1_sem, s2_sem, r2_sem, s3_sem, r3_sem,
):
    sec = lax.axis_index("section")
    band = lax.axis_index("band")
    nsec = lax.axis_size("section")
    nband = lax.axis_size("band")
    y = lax.rem(band, NY)
    z = lax.rem(lax.div(band, NY), NZ)
    x = lax.div(band, NY * NZ)
    next_sec = lax.rem(sec + 1, nsec)
    prev_sec = lax.rem(sec + nsec - 1, nsec)
    up = lax.rem(band + nband - 1, nband)
    down = lax.rem(band + 1, nband)

    def x_peer(d):
        return (sec, (lax.rem(x + d, NX) * NZ + z) * NY + y)

    def y_peer(d):
        return (sec, (x * NZ + z) * NY + lax.rem(y + d, NY))

    z_peer = (sec, (x * NZ + (1 - z)) * NY + y)

    loads = [
        pltpu.make_async_copy(value, raw.at[i], load_sem.at[i])
        for i, value in enumerate((saved, sent_grad, carried, loss_grad, image))
    ]
    loads += [
        pltpu.make_async_copy(first_hbm, first_t, load_sem.at[5]),
        pltpu.make_async_copy(second_hbm, second_t, load_sem.at[6]),
    ]
    for copy in loads:
        copy.start()

    peers = [(next_sec, band), (next_sec, up), (next_sec, down)]
    peers += [(prev_sec, band), (prev_sec, up), (prev_sec, down)]
    peers += [(sec, up), (sec, down), z_peer]
    peers += [x_peer(d) for d in (1, 2, 3)] + [y_peer(d) for d in (1, 2, 3)]
    barrier = pltpu.get_barrier_semaphore()
    for peer in peers:
        pl.semaphore_signal(barrier, inc=1, device_id=peer, device_id_type=MESH)

    def pack_map(i, target, start):
        for r in range(H):
            target[start + r, pl.ds(0, W), :] = raw[i, r, :, pl.ds(0, MAIN)]
            rest = raw[i, r, :, pl.ds(MAIN, C - MAIN)].astype(F32)
            for j in range(2):
                one, two = rest[2 * j * Q : (2 * j + 1) * Q], rest[(2 * j + 1) * Q : (2 * j + 2) * Q]
                pair = jnp.concatenate([one, two], axis=1)
                target[start + r, pl.ds(W, Q), pl.ds(128 * j, 128)] = pair.astype(BF16)

    loads[0].wait()
    pack_map(0, sh, 1)
    loads[1].wait()
    pack_map(1, gsend, 0)
    loads[2].wait()
    pack_map(2, xsend, 0)
    loads[3].wait()
    loads[4].wait()

    @pl.when(sec == nsec - 1)
    def _():
        pack_map(3, gh, 1)

    @pl.when(sec == 0)
    def _():
        pack_map(4, xh, 1)

    pl.semaphore_wait(barrier, len(peers))

    def remote(src, dst, send_sem, recv_sem, peer):
        return pltpu.make_async_remote_copy(
            src_ref=src, dst_ref=dst, send_sem=send_sem, recv_sem=recv_sem,
            device_id=peer, device_id_type=MESH,
        )

    def halos(src, held, to, k):
        return [
            remote(src.at[H - 1], held.at[0], halo_send.at[k], halo_recv.at[k], (to, down)),
            remote(src.at[0], held.at[H + 1], halo_send.at[k + 1], halo_recv.at[k + 1], (to, up)),
        ]

    def shifted_map(src, held, to, k):
        return halos(src, held, to, k) + [
            remote(src, held.at[pl.ds(1, H)], halo_send.at[k + 2], halo_recv.at[k + 2], (to, band))
        ]

    def start_all(copies):
        for copy in copies:
            copy.start()

    def wait_all(copies):
        for copy in copies:
            copy.wait()

    saved_halo = halos(sh.at[pl.ds(1, H)], sh, sec, 0)
    start_all(saved_halo)

    def start_map(src, held, to, k, edge):
        @pl.when(sec == edge)
        def _():
            start_all(halos(held.at[pl.ds(1, H)], held, sec, k + 3))

        @pl.when(sec != nsec - 1 - edge)
        def _():
            start_all(shifted_map(src, held, to, k))

    def wait_map(src, held, to, k, edge):
        copies = shifted_map(src, held, to, k)

        @pl.when(sec != nsec - 1 - edge)
        def _():
            for copy in copies:
                copy.wait_send()

        @pl.when(sec == edge)
        def _():
            wait_all(halos(held.at[pl.ds(1, H)], held, sec, k + 3))

        @pl.when(sec != edge)
        def _():
            for copy in copies:
                copy.wait_recv()

    g_map = (gsend, gh, prev_sec, 2, nsec - 1)
    x_map = (xsend, xh, next_sec, 7, 0)
    start_map(*g_map)

    def turn(source, target):
        for k in range(0, 9 * C, 640):
            n = min(640, 9 * C - k)
            target[pl.ds(k, n), :] = jnp.transpose(source[:, pl.ds(k, n)])

    loads[5].wait()
    turn(first_t, first)
    loads[6].wait()
    turn(second_t, second)

    terms[pl.ds(9 * C, 8), :] = jnp.zeros((8, CL), F32)
    terms[:, pl.ds(MAIN, CL - MAIN)] = jnp.zeros((9 * C + 8, CL - MAIN), F32)
    shift_buf[pl.ds(0, 8), :] = jnp.zeros((8, CL), F32)
    shift_buf[pl.ds(8 + 4 * W, 8), :] = jnp.zeros((8, CL), F32)
    column = lax.broadcasted_iota(jnp.int32, (W, C), 0)

    def build(held, out):
        for r in range(H + 2):
            main = held[r, pl.ds(0, W), :]
            pairs = [held[r, pl.ds(W, Q), pl.ds(128 * j, 128)].astype(F32) for j in range(2)]
            rest = jnp.concatenate(
                [part for pair in pairs for part in (pair, pltpu.roll(pair, 64, 1))], axis=0
            )
            outside = None
            if r == 0:
                outside = band == 0
            if r == H + 1:
                outside = band == nband - 1
            if outside is not None:
                main = jnp.where(outside, jnp.zeros_like(main), main)
                rest = jnp.where(outside, jnp.zeros_like(rest), rest)
            rows = pl.ds(8 + r * W, W)
            shift_buf[rows, pl.ds(0, MAIN)] = main.astype(F32)
            shift_buf[rows, pl.ds(MAIN, 128)] = rest
            out[1, pl.ds(r * W, W), :] = shift_buf[rows, pl.ds(0, C)].astype(BF16)
        for r in range(H + 2):
            low = shift_buf[pl.ds(7 + r * W, W), pl.ds(0, C)]
            out[0, pl.ds(r * W, W), :] = jnp.where(column == 0, 0.0, low).astype(BF16)
            high = shift_buf[pl.ds(9 + r * W, W), pl.ds(0, C)]
            out[2, pl.ds(r * W, W), :] = jnp.where(column == W - 1, 0.0, high).astype(BF16)

    def conv(maps, weights):
        total = None
        for tap in range(9):
            ky, kx = divmod(tap, 3)
            part = dot(maps[kx, pl.ds(ky * W, M), :], weights[pl.ds(tap * C, C), :])
            total = part if total is None else total + part
        return total

    def conv_t(maps, weights):
        total = None
        for tap in range(9):
            ky, kx = divmod(tap, 3)
            part = dot_t(maps[2 - kx, pl.ds((2 - ky) * W, M), :], weights[pl.ds(tap * C, C), :])
            total = part if total is None else total + part
        return total

    def wgrad(vt, maps):
        for tap in range(9):
            ky, kx = divmod(tap, 3)
            terms[pl.ds(tap * C, C), pl.ds(0, C)] = dot(
                vt[...], maps[2 - kx, pl.ds((2 - ky) * W, M), :]
            )

    lane = lax.broadcasted_iota(jnp.int32, (PR, 128), 1)

    def pack(k):
        for half in range(2):
            for dest in range(4):
                rests = []
                for j in range(4):
                    xx, yy = (dest, j) if half == 0 else (j, dest)
                    row = ((xx * NZ + half) * NY + yy) * PIECE
                    send1[k, half, dest, pl.ds(j * PR, PR), :] = terms[
                        pl.ds(row, PR), pl.ds(0, MAIN)
                    ].astype(BF16)
                    rests.append(terms[pl.ds(row, PR), pl.ds(MAIN, 128)])
                for j in range(2):
                    pair = jnp.where(
                        lane < 64, rests[2 * j], pltpu.roll(rests[2 * j + 1], 64, 1)
                    )
                    send1[k, half, dest, pl.ds(4 * PR, PR), pl.ds(j * 128, 128)] = pair.astype(BF16)

    low, high = pl.ds(0, SEND // 2), pl.ds(SEND // 2, SEND // 2)

    def stage1(k):
        relays, plain, added = [], [], []
        for half, (pos, peer) in enumerate(((x, x_peer), (y, y_peer))):
            for side, (d, via, own) in enumerate(((1, low, high), (3, high, low))):
                def copy(ahead, rows, dst, i):
                    return remote(
                        send1.at[k, half, lax.rem(pos + ahead, 4), rows], dst,
                        s1_sem.at[k, half, i + side], r1_sem.at[k, half, i + side], peer(d),
                    )

                relays.append(copy(2, via, relay.at[k, half, side], 0))
                plain.append(copy(d, own, recv1.at[k, half, side, own], 2))
                added.append(copy(d, via, recv1.at[k, half, side, via], 4))
        return relays, plain, added

    def add_relays(k):
        for half, pos in enumerate((x, y)):
            for side, (d, via) in enumerate(((1, low), (3, high))):
                ahead = lax.rem(pos + d, 4)
                send1[k, half, ahead, via, :] = (
                    send1[k, half, ahead, via, :].astype(F32) + relay[k, half, side].astype(F32)
                ).astype(BF16)

    def stage2(k):
        copies = []
        for d in (1, 3, 2):
            for half, (pos, peer) in enumerate(((y, y_peer), (x, x_peer))):
                copies.append(
                    remote(
                        send2.at[k, half, lax.rem(pos + d, 4)], recv2.at[k, half, d - 1],
                        s2_sem.at[k, half, d - 1], r2_sem.at[k, half, d - 1], peer(d),
                    )
                )
        return copies

    def sum1(k):
        for half, pos in enumerate((x, y)):
            def total(rows, lanes):
                value = send1[k, half, pos, rows, lanes].astype(F32)
                for d in range(2):
                    value = value + recv1[k, half, d, rows, lanes].astype(F32)
                return value

            for j in range(4):
                main = total(pl.ds(j * PR, PR), pl.ds(0, MAIN))
                held2[k, half, j, :, pl.ds(0, MAIN)] = main
                send2[k, half, j, :, pl.ds(0, MAIN)] = main.astype(BF16)
            for j in range(2):
                rest = total(pl.ds(4 * PR, PR), pl.ds(j * 128, 128))
                for i, part in enumerate((rest, pltpu.roll(rest, 64, 1))):
                    held2[k, half, 2 * j + i, :, pl.ds(MAIN, 128)] = part
                    send2[k, half, 2 * j + i, :, pl.ds(MAIN, 128)] = part.astype(BF16)

    def sum2(k):
        sums = []
        for half, pos in enumerate((y, x)):
            value = held2[k, half, pos]
            for d in range(3):
                value = value + recv2[k, half, d].astype(F32)
            sums.append(value)
        keep3[k] = jnp.where(z == 0, sums[0], sums[1])
        send3[k] = jnp.where(z == 0, sums[1], sums[0]).astype(BF16)

    def stage3(k):
        return remote(send3.at[k], recv3.at[k], s3_sem.at[k], r3_sem.at[k], z_peer)

    wait_all(saved_halo)
    build(sh, ss)
    pre = conv(ss, first)
    sig = jax.nn.sigmoid(pre)
    actt[...] = jnp.transpose(pre * sig).astype(BF16)
    slope[...] = sig * (1.0 + pre * (1.0 - sig))
    wait_map(*g_map)
    start_map(*x_map)
    build(gh, gs)
    wgrad(actt, gs)
    pack(1)
    second_relays, second_plain, second_added = stage1(1)
    start_all(second_relays + second_plain)

    grad_pre = (conv_t(gs, second) * slope[...]).astype(BF16)
    for r in range(H):
        raw[0, r] = grad_pre[r * W : (r + 1) * W]
    pack_map(0, ph, 1)
    pre_halo = halos(ph.at[pl.ds(1, H)], ph, sec, 12)
    start_all(pre_halo)

    for tap in range(9):
        ky, kx = divmod(tap, 3)
        terms[pl.ds(tap * C, C), pl.ds(0, C)] = dot(
            jnp.transpose(ss[kx, pl.ds(ky * W, M), :]), grad_pre
        )
    wait_all(second_relays)
    add_relays(1)
    start_all(second_added)
    pack(0)
    first_relays, first_plain, first_added = stage1(0)
    start_all(first_relays + first_plain)

    wait_all(first_relays)
    add_relays(0)
    start_all(first_added)

    wait_all(second_plain + second_added)
    sum1(1)
    second_2 = stage2(1)
    start_all(second_2)

    wait_map(*x_map)
    build(xh, xs)
    pre = conv(xs, first)
    act = (pre * jax.nn.sigmoid(pre)).astype(BF16)
    for r in range(H):
        raw[1, r] = act[r * W : (r + 1) * W]
    pack_map(1, ah, 1)
    act_halo = halos(ah.at[pl.ds(1, H)], ah, sec, 14)
    start_all(act_halo)

    wait_all(first_plain + first_added)
    sum1(0)
    first_2 = stage2(0)
    start_all(first_2)

    wait_all(pre_halo)
    build(ph, ps)
    igrad_flat = conv_t(ps, first)
    for r in range(H):
        igrad[r] = (gs[1, pl.ds((1 + r) * W, W), :].astype(F32) + igrad_flat[r * W : (r + 1) * W]).astype(BF16)

    wait_all(second_2)
    sum2(1)
    second_3 = stage3(1)
    second_3.start()

    wait_all(first_2)
    sum2(0)
    first_3 = stage3(0)
    first_3.start()

    wait_all(act_halo)
    build(ah, as_)
    out_flat = conv(as_, second)
    for r in range(H):
        fwd[r] = (xs[1, pl.ds((1 + r) * W, W), :].astype(F32) + out_flat[r * W : (r + 1) * W]).astype(BF16)

    for k, copy, out in ((1, second_3, gsecond), (0, first_3, gfirst)):
        copy.wait()
        out[...] = (keep3[k] + recv3[k].astype(F32))[:PIECE, :C] * factor


def copy_out(fwd, igrad, gfirst, gsecond, fwd_out, igrad_out, gfirst_out, gsecond_out):
    fwd_out[...] = fwd[...]
    igrad_out[...] = igrad[...]
    gfirst_out[...] = gfirst[...].reshape(PIECE, 1, C)
    gsecond_out[...] = gsecond[...].reshape(PIECE, 1, C)


def body(image, carried, saved, sent_grad, loss_grad, first_kernel, second_kernel):
    factor = 1.0 / math.sqrt(H * lax.axis_size("band") * W)
    any_spec = pl.BlockSpec(memory_space=pl.ANY)
    vmem_spec = pl.BlockSpec(memory_space=pltpu.VMEM)
    vmem, dma = pltpu.VMEM, pltpu.SemaphoreType.DMA
    halo_map = vmem((H + 2, ROW, MAIN), BF16)
    moved = vmem((3, (H + 2) * W, C), BF16)
    fwd, igrad, gfirst, gsecond = pl.pallas_call(
        functools.partial(kernel, factor),
        out_shape=(
            vmem((H, W, C), BF16), vmem((H, W, C), BF16), vmem((PIECE, C), F32), vmem((PIECE, C), F32),
        ),
        in_specs=[any_spec] * 7,
        out_specs=(vmem_spec,) * 4,
        scratch_shapes=[
            vmem((C, 9 * C), BF16), vmem((C, 9 * C), BF16),
            vmem((9 * C, C), BF16), vmem((9 * C, C), BF16),
            vmem((5, H, W, C), BF16), vmem((H, ROW, MAIN), BF16), vmem((H, ROW, MAIN), BF16),
            halo_map, halo_map, halo_map, halo_map, halo_map,
            moved, moved, moved, moved, moved,
            vmem((16 + (H + 2) * W, CL), F32),
            vmem((M, C), F32),
            vmem((C, M), BF16),
            vmem((9 * C + 8, CL), F32),
            vmem((2, 2, 4, SEND, MAIN), BF16), vmem((2, 2, 2, SEND // 2, MAIN), BF16),
            vmem((2, 2, 2, SEND, MAIN), BF16),
            vmem((2, 2, 4, PR, CL), F32), vmem((2, 2, 4, PR, CL), BF16),
            vmem((2, 2, 3, PR, CL), BF16),
            vmem((2, PR, CL), BF16), vmem((2, PR, CL), BF16), vmem((2, PR, CL), F32),
            dma((7,)), dma((16,)), dma((16,)),
            dma((2, 2, 6)), dma((2, 2, 6)), dma((2, 2, 3)), dma((2, 2, 3)),
            dma((2,)), dma((2,)),
        ],
        compiler_params=pltpu.CompilerParams(
            collective_id=0, has_side_effects=True, vmem_limit_bytes=56 * 1024 * 1024
        ),
    )(image, carried[0], saved[0], sent_grad[0], loss_grad, first_kernel[0].T, second_kernel[0].T)
    map_shape = jax.ShapeDtypeStruct((H, W, C), BF16)
    grad_shape = jax.ShapeDtypeStruct((PIECE, 1, C), F32)
    fwd, igrad, gfirst, gsecond = pl.pallas_call(
        copy_out,
        out_shape=(map_shape, map_shape, grad_shape, grad_shape),
        in_specs=[vmem_spec] * 4,
        out_specs=(vmem_spec,) * 4,
    )(*[pltpu.with_memory_space_constraint(v, pltpu.VMEM) for v in (fwd, igrad, gfirst, gsecond)])
    return fwd[None], igrad[None], gfirst.reshape(1, PIECE, C), gsecond.reshape(1, PIECE, C)


def solution(mesh):
    return jax.shard_map(
        body,
        mesh=mesh,
        in_specs=(
            P("band", None, None),
            P("section", "band", None, None),
            P("section", "band", None, None),
            P("section", "band", None, None),
            P("band", None, None),
            P("section", None, None),
            P("section", None, None),
        ),
        out_specs=(
            P("section", "band", None, None),
            P("section", "band", None, None),
            P("section", "band", None),
            P("section", "band", None),
        ),
        check_vma=False,
    )
```

```python
import functools
import math

import jax
import jax.numpy as jnp
from jax import lax
from jax.experimental import pallas as pl
from jax.experimental.pallas import tpu as pltpu
from jax.sharding import PartitionSpec as P

MESH = pl.DeviceIdType.MESH
BF16 = jnp.bfloat16
F32 = jnp.float32

H, W, C = 2, 160, 320
M = H * W
CL = 384
PIECE = 90
PR = 96
MAIN = 256
SEND = 5 * PR
PQ = PR // 4
Q = W // 4
ROW = W + Q
NX, NY, NZ = 4, 4, 2


def dot(a, b):
    return jnp.dot(a, b, preferred_element_type=F32)


def dot_t(a, b):
    return lax.dot_general(a, b, (((1,), (1,)), ((), ())), preferred_element_type=F32)


def kernel(
    factor, image, carried, saved, sent_grad, loss_grad, first_hbm, second_hbm,
    fwd, igrad, gfirst, gsecond,
    first_t, second_t, first, second, raw, gsend, xsend, xh, sh, gh, ah, ph, xs, ss, gs, as_, ps, shift_buf, slope, actt,
    terms, send1, relay, recv1, held2, send2, recv2, send3, recv3, keep3,
    load_sem, halo_send, halo_recv, s1_sem, r1_sem, s2_sem, r2_sem, s3_sem, r3_sem,
):
    sec = lax.axis_index("section")
    band = lax.axis_index("band")
    nsec = lax.axis_size("section")
    nband = lax.axis_size("band")
    y = lax.rem(band, NY)
    z = lax.rem(lax.div(band, NY), NZ)
    x = lax.div(band, NY * NZ)
    next_sec = lax.rem(sec + 1, nsec)
    prev_sec = lax.rem(sec + nsec - 1, nsec)
    up = lax.rem(band + nband - 1, nband)
    down = lax.rem(band + 1, nband)

    def x_peer(d):
        return (sec, (lax.rem(x + d, NX) * NZ + z) * NY + y)

    def y_peer(d):
        return (sec, (x * NZ + z) * NY + lax.rem(y + d, NY))

    z_peer = (sec, (x * NZ + (1 - z)) * NY + y)

    loads = [
        pltpu.make_async_copy(value, raw.at[i], load_sem.at[i])
        for i, value in enumerate((saved, sent_grad, carried, loss_grad, image))
    ]
    loads += [
        pltpu.make_async_copy(first_hbm, first_t, load_sem.at[5]),
        pltpu.make_async_copy(second_hbm, second_t, load_sem.at[6]),
    ]
    for copy in loads:
        copy.start()

    peers = [(next_sec, band), (next_sec, up), (next_sec, down)]
    peers += [(prev_sec, band), (prev_sec, up), (prev_sec, down)]
    peers += [(sec, up), (sec, down), z_peer]
    peers += [x_peer(d) for d in (1, 2, 3)] + [y_peer(d) for d in (1, 2, 3)]
    barrier = pltpu.get_barrier_semaphore()
    for peer in peers:
        pl.semaphore_signal(barrier, inc=1, device_id=peer, device_id_type=MESH)

    def pack_map(i, target, start):
        for r in range(H):
            target[start + r, pl.ds(0, W), :] = raw[i, r, :, pl.ds(0, MAIN)]
            rest = raw[i, r, :, pl.ds(MAIN, C - MAIN)].astype(F32)
            for j in range(2):
                one, two = rest[2 * j * Q : (2 * j + 1) * Q], rest[(2 * j + 1) * Q : (2 * j + 2) * Q]
                pair = jnp.concatenate([one, two], axis=1)
                target[start + r, pl.ds(W, Q), pl.ds(128 * j, 128)] = pair.astype(BF16)

    loads[0].wait()
    pack_map(0, sh, 1)
    loads[1].wait()
    pack_map(1, gsend, 0)
    loads[3].wait()

    @pl.when(sec == nsec - 1)
    def _():
        pack_map(3, gh, 1)

    pl.semaphore_wait(barrier, len(peers))

    def remote(src, dst, send_sem, recv_sem, peer):
        return pltpu.make_async_remote_copy(
            src_ref=src, dst_ref=dst, send_sem=send_sem, recv_sem=recv_sem,
            device_id=peer, device_id_type=MESH,
        )

    def halos(src, held, to, k):
        return [
            remote(src.at[H - 1], held.at[0], halo_send.at[k], halo_recv.at[k], (to, down)),
            remote(src.at[0], held.at[H + 1], halo_send.at[k + 1], halo_recv.at[k + 1], (to, up)),
        ]

    def shifted_map(src, held, to, k):
        return halos(src, held, to, k) + [
            remote(src, held.at[pl.ds(1, H)], halo_send.at[k + 2], halo_recv.at[k + 2], (to, band))
        ]

    def start_all(copies):
        for copy in copies:
            copy.start()

    def wait_all(copies):
        for copy in copies:
            copy.wait()

    saved_halo = halos(sh.at[pl.ds(1, H)], sh, sec, 0)
    start_all(saved_halo)

    def start_map(src, held, to, k, edge):
        @pl.when(sec == edge)
        def _():
            start_all(halos(held.at[pl.ds(1, H)], held, sec, k + 3))

        @pl.when(sec != nsec - 1 - edge)
        def _():
            start_all(shifted_map(src, held, to, k))

    def wait_map(src, held, to, k, edge):
        copies = shifted_map(src, held, to, k)

        @pl.when(sec != nsec - 1 - edge)
        def _():
            for copy in copies:
                copy.wait_send()

        @pl.when(sec == edge)
        def _():
            wait_all(halos(held.at[pl.ds(1, H)], held, sec, k + 3))

        @pl.when(sec != edge)
        def _():
            for copy in copies:
                copy.wait_recv()

    g_map = (gsend, gh, prev_sec, 2, nsec - 1)
    x_map = (xsend, xh, next_sec, 7, 0)
    start_map(*g_map)

    loads[2].wait()
    pack_map(2, xsend, 0)
    loads[4].wait()

    @pl.when(sec == 0)
    def _():
        pack_map(4, xh, 1)

    def turn(source, target):
        for k in range(0, 9 * C, 640):
            n = min(640, 9 * C - k)
            target[pl.ds(k, n), :] = jnp.transpose(source[:, pl.ds(k, n)])

    loads[5].wait()
    turn(first_t, first)
    loads[6].wait()
    turn(second_t, second)

    terms[pl.ds(9 * C, 8), :] = jnp.zeros((8, CL), F32)
    terms[:, pl.ds(MAIN, CL - MAIN)] = jnp.zeros((9 * C + 8, CL - MAIN), F32)
    shift_buf[pl.ds(0, 8), :] = jnp.zeros((8, CL), F32)
    shift_buf[pl.ds(8 + 4 * W, 8), :] = jnp.zeros((8, CL), F32)
    column = lax.broadcasted_iota(jnp.int32, (W, C), 0)

    def build(held, out):
        for r in range(H + 2):
            main = held[r, pl.ds(0, W), :]
            pairs = [held[r, pl.ds(W, Q), pl.ds(128 * j, 128)].astype(F32) for j in range(2)]
            rest = jnp.concatenate(
                [part for pair in pairs for part in (pair, pltpu.roll(pair, 64, 1))], axis=0
            )
            outside = None
            if r == 0:
                outside = band == 0
            if r == H + 1:
                outside = band == nband - 1
            if outside is not None:
                main = jnp.where(outside, jnp.zeros_like(main), main)
                rest = jnp.where(outside, jnp.zeros_like(rest), rest)
            rows = pl.ds(8 + r * W, W)
            shift_buf[rows, pl.ds(0, MAIN)] = main.astype(F32)
            shift_buf[rows, pl.ds(MAIN, 128)] = rest
            out[1, pl.ds(r * W, W), :] = shift_buf[rows, pl.ds(0, C)].astype(BF16)
        for r in range(H + 2):
            low = shift_buf[pl.ds(7 + r * W, W), pl.ds(0, C)]
            out[0, pl.ds(r * W, W), :] = jnp.where(column == 0, 0.0, low).astype(BF16)
            high = shift_buf[pl.ds(9 + r * W, W), pl.ds(0, C)]
            out[2, pl.ds(r * W, W), :] = jnp.where(column == W - 1, 0.0, high).astype(BF16)

    def conv(maps, weights):
        total = None
        for tap in range(9):
            ky, kx = divmod(tap, 3)
            part = dot(maps[kx, pl.ds(ky * W, M), :], weights[pl.ds(tap * C, C), :])
            total = part if total is None else total + part
        return total

    def conv_t(maps, weights):
        total = None
        for tap in range(9):
            ky, kx = divmod(tap, 3)
            part = dot_t(maps[2 - kx, pl.ds((2 - ky) * W, M), :], weights[pl.ds(tap * C, C), :])
            total = part if total is None else total + part
        return total

    def wgrad(vt, maps):
        for tap in range(9):
            ky, kx = divmod(tap, 3)
            terms[pl.ds(tap * C, C), pl.ds(0, C)] = dot(
                vt[...], maps[2 - kx, pl.ds((2 - ky) * W, M), :]
            )

    lane = lax.broadcasted_iota(jnp.int32, (PR, 128), 1)

    def pack(k):
        for half in range(2):
            for dest in range(4):
                rests = []
                for j in range(4):
                    xx, yy = (dest, j) if half == 0 else (j, dest)
                    row = ((xx * NZ + half) * NY + yy) * PIECE
                    send1[k, half, dest, pl.ds(j * PR, PR), :] = terms[
                        pl.ds(row, PR), pl.ds(0, MAIN)
                    ].astype(BF16)
                    rests.append(terms[pl.ds(row, PR), pl.ds(MAIN, 128)])
                for j in range(2):
                    pair = jnp.where(
                        lane < 64, rests[2 * j], pltpu.roll(rests[2 * j + 1], 64, 1)
                    )
                    send1[k, half, dest, pl.ds(4 * PR, PR), pl.ds(j * 128, 128)] = pair.astype(BF16)

    low, high = pl.ds(0, SEND // 2), pl.ds(SEND // 2, SEND // 2)

    def stage1(k):
        relays, plain, added = [], [], []
        for half, (pos, peer) in enumerate(((x, x_peer), (y, y_peer))):
            for side, (d, via, own) in enumerate(((1, low, high), (3, high, low))):
                def copy(ahead, rows, dst, i):
                    return remote(
                        send1.at[k, half, lax.rem(pos + ahead, 4), rows], dst,
                        s1_sem.at[k, half, i + side], r1_sem.at[k, half, i + side], peer(d),
                    )

                relays.append(copy(2, via, relay.at[k, half, side], 0))
                plain.append(copy(d, own, recv1.at[k, half, side, own], 2))
                added.append(copy(d, via, recv1.at[k, half, side, via], 4))
        return relays, plain, added

    def add_relays(k):
        for half, pos in enumerate((x, y)):
            for side, (d, via) in enumerate(((1, low), (3, high))):
                ahead = lax.rem(pos + d, 4)
                send1[k, half, ahead, via, :] = (
                    send1[k, half, ahead, via, :].astype(F32) + relay[k, half, side].astype(F32)
                ).astype(BF16)

    def stage2(k):
        copies = []
        for d in (1, 3, 2):
            for half, (pos, peer) in enumerate(((y, y_peer), (x, x_peer))):
                copies.append(
                    remote(
                        send2.at[k, half, lax.rem(pos + d, 4)], recv2.at[k, half, d - 1],
                        s2_sem.at[k, half, d - 1], r2_sem.at[k, half, d - 1], peer(d),
                    )
                )
        return copies

    def sum1(k):
        for half, pos in enumerate((x, y)):
            def total(rows, lanes):
                value = send1[k, half, pos, rows, lanes].astype(F32)
                for d in range(2):
                    value = value + recv1[k, half, d, rows, lanes].astype(F32)
                return value

            for j in range(4):
                main = total(pl.ds(j * PR, PR), pl.ds(0, MAIN))
                held2[k, half, j, :, pl.ds(0, MAIN)] = main
                send2[k, half, j, pl.ds(0, PR), :] = main.astype(BF16)
            for j in range(2):
                rest = total(pl.ds(4 * PR, PR), pl.ds(j * 128, 128))
                for i, part in enumerate((rest, pltpu.roll(rest, 64, 1))):
                    held2[k, half, 2 * j + i, :, pl.ds(MAIN, 128)] = part
                    for p in range(2):
                        one, two = part[2 * p * PQ : (2 * p + 1) * PQ], part[(2 * p + 1) * PQ : (2 * p + 2) * PQ]
                        pair = jnp.where(lane[:PQ] < 64, one, pltpu.roll(two, 64, 1))
                        send2[k, half, 2 * j + i, pl.ds(PR, PQ), pl.ds(128 * p, 128)] = pair.astype(BF16)

    def sum2(k):
        sums = []
        for half, pos in enumerate((y, x)):
            main, rest = held2[k, half, pos, :, pl.ds(0, MAIN)], held2[k, half, pos, :, pl.ds(MAIN, 128)]
            pairs = []
            for p in range(2):
                pairs.append(jnp.zeros((PQ, 128), F32))
                for d in range(3):
                    pairs[p] = pairs[p] + recv2[k, half, d, pl.ds(PR, PQ), pl.ds(128 * p, 128)].astype(F32)
            for d in range(3):
                main = main + recv2[k, half, d, pl.ds(0, PR), :].astype(F32)
            rest = rest + jnp.concatenate(
                [part for pair in pairs for part in (pair, pltpu.roll(pair, 64, 1))], axis=0
            )
            sums.append(jnp.concatenate([main, rest], axis=1))
        keep3[k] = jnp.where(z == 0, sums[0], sums[1])
        send3[k] = jnp.where(z == 0, sums[1], sums[0]).astype(BF16)

    def stage3(k):
        return remote(send3.at[k], recv3.at[k], s3_sem.at[k], r3_sem.at[k], z_peer)

    wait_all(saved_halo)
    build(sh, ss)
    pre = conv(ss, first)
    sig = jax.nn.sigmoid(pre)
    actt[...] = jnp.transpose(pre * sig).astype(BF16)
    slope[...] = sig * (1.0 + pre * (1.0 - sig))
    wait_map(*g_map)
    start_map(*x_map)
    build(gh, gs)
    wgrad(actt, gs)
    pack(1)
    second_relays, second_plain, second_added = stage1(1)
    start_all(second_relays + second_plain)

    grad_pre = (conv_t(gs, second) * slope[...]).astype(BF16)
    for r in range(H):
        raw[0, r] = grad_pre[r * W : (r + 1) * W]
    pack_map(0, ph, 1)
    pre_halo = halos(ph.at[pl.ds(1, H)], ph, sec, 12)
    start_all(pre_halo)

    for tap in range(9):
        ky, kx = divmod(tap, 3)
        terms[pl.ds(tap * C, C), pl.ds(0, C)] = dot(
            jnp.transpose(ss[kx, pl.ds(ky * W, M), :]), grad_pre
        )
    wait_all(second_relays)
    add_relays(1)
    start_all(second_added)
    pack(0)
    first_relays, first_plain, first_added = stage1(0)
    start_all(first_relays + first_plain)

    wait_all(first_relays)
    add_relays(0)
    start_all(first_added)

    wait_all(second_plain + second_added)
    sum1(1)
    second_2 = stage2(1)
    start_all(second_2)

    wait_map(*x_map)
    build(xh, xs)
    pre = conv(xs, first)
    act = (pre * jax.nn.sigmoid(pre)).astype(BF16)
    for r in range(H):
        raw[1, r] = act[r * W : (r + 1) * W]
    pack_map(1, ah, 1)
    act_halo = halos(ah.at[pl.ds(1, H)], ah, sec, 14)
    start_all(act_halo)

    wait_all(first_plain + first_added)
    sum1(0)
    first_2 = stage2(0)
    start_all(first_2)

    wait_all(second_2)
    sum2(1)
    second_3 = stage3(1)
    second_3.start()

    wait_all(pre_halo)
    build(ph, ps)
    igrad_flat = conv_t(ps, first)
    for r in range(H):
        igrad[r] = (gs[1, pl.ds((1 + r) * W, W), :].astype(F32) + igrad_flat[r * W : (r + 1) * W]).astype(BF16)

    wait_all(first_2)
    sum2(0)
    first_3 = stage3(0)
    first_3.start()

    wait_all(act_halo)
    build(ah, as_)
    out_flat = conv(as_, second)
    for r in range(H):
        fwd[r] = (xs[1, pl.ds((1 + r) * W, W), :].astype(F32) + out_flat[r * W : (r + 1) * W]).astype(BF16)

    for k, copy, out in ((1, second_3, gsecond), (0, first_3, gfirst)):
        copy.wait()
        out[...] = (keep3[k] + recv3[k].astype(F32))[:PIECE, :C] * factor


def copy_out(fwd, igrad, gfirst, gsecond, fwd_out, igrad_out, gfirst_out, gsecond_out):
    fwd_out[...] = fwd[...]
    igrad_out[...] = igrad[...]
    gfirst_out[...] = gfirst[...].reshape(PIECE, 1, C)
    gsecond_out[...] = gsecond[...].reshape(PIECE, 1, C)


def body(image, carried, saved, sent_grad, loss_grad, first_kernel, second_kernel):
    factor = 1.0 / math.sqrt(H * lax.axis_size("band") * W)
    any_spec = pl.BlockSpec(memory_space=pl.ANY)
    vmem_spec = pl.BlockSpec(memory_space=pltpu.VMEM)
    vmem, dma = pltpu.VMEM, pltpu.SemaphoreType.DMA
    halo_map = vmem((H + 2, ROW, MAIN), BF16)
    moved = vmem((3, (H + 2) * W, C), BF16)
    fwd, igrad, gfirst, gsecond = pl.pallas_call(
        functools.partial(kernel, factor),
        out_shape=(
            vmem((H, W, C), BF16), vmem((H, W, C), BF16), vmem((PIECE, C), F32), vmem((PIECE, C), F32),
        ),
        in_specs=[any_spec] * 7,
        out_specs=(vmem_spec,) * 4,
        scratch_shapes=[
            vmem((C, 9 * C), BF16), vmem((C, 9 * C), BF16),
            vmem((9 * C, C), BF16), vmem((9 * C, C), BF16),
            vmem((5, H, W, C), BF16), vmem((H, ROW, MAIN), BF16), vmem((H, ROW, MAIN), BF16),
            halo_map, halo_map, halo_map, halo_map, halo_map,
            moved, moved, moved, moved, moved,
            vmem((16 + (H + 2) * W, CL), F32),
            vmem((M, C), F32),
            vmem((C, M), BF16),
            vmem((9 * C + 8, CL), F32),
            vmem((2, 2, 4, SEND, MAIN), BF16), vmem((2, 2, 2, SEND // 2, MAIN), BF16),
            vmem((2, 2, 2, SEND, MAIN), BF16),
            vmem((2, 2, 4, PR, CL), F32), vmem((2, 2, 4, PR + PQ, MAIN), BF16),
            vmem((2, 2, 3, PR + PQ, MAIN), BF16),
            vmem((2, PR, CL), BF16), vmem((2, PR, CL), BF16), vmem((2, PR, CL), F32),
            dma((7,)), dma((16,)), dma((16,)),
            dma((2, 2, 6)), dma((2, 2, 6)), dma((2, 2, 3)), dma((2, 2, 3)),
            dma((2,)), dma((2,)),
        ],
        compiler_params=pltpu.CompilerParams(
            collective_id=0, has_side_effects=True, vmem_limit_bytes=56 * 1024 * 1024
        ),
    )(image, carried[0], saved[0], sent_grad[0], loss_grad, first_kernel[0].T, second_kernel[0].T)
    map_shape = jax.ShapeDtypeStruct((H, W, C), BF16)
    grad_shape = jax.ShapeDtypeStruct((PIECE, 1, C), F32)
    fwd, igrad, gfirst, gsecond = pl.pallas_call(
        copy_out,
        out_shape=(map_shape, map_shape, grad_shape, grad_shape),
        in_specs=[vmem_spec] * 4,
        out_specs=(vmem_spec,) * 4,
    )(*[pltpu.with_memory_space_constraint(v, pltpu.VMEM) for v in (fwd, igrad, gfirst, gsecond)])
    return fwd[None], igrad[None], gfirst.reshape(1, PIECE, C), gsecond.reshape(1, PIECE, C)


def solution(mesh):
    return jax.shard_map(
        body,
        mesh=mesh,
        in_specs=(
            P("band", None, None),
            P("section", "band", None, None),
            P("section", "band", None, None),
            P("section", "band", None, None),
            P("band", None, None),
            P("section", None, None),
            P("section", None, None),
        ),
        out_specs=(
            P("section", "band", None, None),
            P("section", "band", None, None),
            P("section", "band", None),
            P("section", "band", None),
        ),
        check_vma=False,
    )
```
